32 devices in a mesh: groups: 2 (over y), ctx: 4 (over z), kvh: 2 (over x), sub: 2 (over core).
Axes of the slice: x: 2, y: 2, z: 4, core: 2. Of those that a mesh axis runs over, the one named last changes fastest.
Arguments:
- queries: bfloat16 [2048, 64, 128], P(('groups', 'ctx', 'sub'), 'kvh'), parts along dimension 0, may hold values from -8 to 8
- key_states: bfloat16 [1024, 8, 128], P(('groups', 'ctx'), 'kvh'), parts along dimension 0, may hold values from -8 to 8
- obs_positions: int32 [2048], P(('groups', 'ctx', 'sub')), parts along dimension 0, may hold values from 0 to 511, as said below
- block_lists: int32 [16, 8], P(('groups', 'ctx', 'sub')), parts along dimension 0, may hold values from -1 to 7, as said below
- bin_edges: int32 [258], P('groups'), parts along dimension 0, may hold values from 0 to 512, as said below
Outputs:
- key_mass: float32 [8, 1024], P('kvh', ('groups', 'ctx')), parts along dimension 1
- bin_density: float32 [8, 256], P('kvh', 'groups'), parts along dimension 1
The draws below stay inside these ranges and needn't reach their ends.
There are 2 independent parts, one for each index of `groups`. The reference program is written for one: setup_inputs(seed, part) draws one part's arguments, and reference() takes and returns one part's arrays. A program takes and returns all parts, laid end to end along the dimension named above; each array names one. Nothing has to cross between parts.
Inputs may be any that keep to these rules, and one draw needn't show every extreme that they name: `obs_positions`: each aligned block of 128 entries holds distinct positions in increasing order. `block_lists`: each row names 1 to 8 distinct key blocks in its first entries and holds -1 in the others; some row names 8. `bin_edges`: strictly increasing from 0 to 512.
All inputs are finite; a program needn't handle non-finite values.
Results may differ from the reference program's by a relative error of at most 0.0003.
Values may be sent and summed in bfloat16 or wider, within the bound.
No kernel may reach another device: no remote copies, remote signals or barrier semaphores. Data moves between devices by JAX's collectives and lax.ppermute only.
A program may use at most 64 MiB of HBM per device.

```python
import jax
import jax.numpy as jnp
from jax import lax

KVH = 8
QPK = 8
HD = 128
OBS_DEV = 128
KB = 64
LIST = 8
NBINS = 128
S = 512
NKB = 8
NQB = 8
OBS = 1024
QH = 64


def obs_table(key):
    base = jax.random.fold_in(key, 101)
    row_keys = jax.random.split(base, NQB)
    picked = jax.vmap(lambda one_key: jax.random.permutation(one_key, S)[:OBS_DEV])(row_keys)
    sorted_rows = jnp.sort(picked, axis=1)
    chosen = jax.random.randint(jax.random.fold_in(base, 7), (2,), 0, NQB)
    sorted_rows = sorted_rows.at[chosen[0], OBS_DEV - 1].set(S - 1)
    sorted_rows = sorted_rows.at[chosen[1], 0].set(0)
    return sorted_rows.astype(jnp.int32)


def draw_key_states(key, part):
    values = jax.random.normal(jax.random.fold_in(key, 202), (S, KVH, HD), jnp.float32)
    return jnp.clip(values, -8.0, 8.0).astype(jnp.bfloat16)


def draw_queries(key, part):
    values = jax.random.normal(jax.random.fold_in(key, 505), (OBS, QH, HD), jnp.float32)
    return jnp.clip(values, -8.0, 8.0).astype(jnp.bfloat16)


def draw_obs_positions(key, part):
    return obs_table(key).reshape(OBS)


def draw_block_lists(key, part):
    base = jax.random.fold_in(key, 303)
    row_keys = jax.random.split(base, NQB + 2)
    picked = jax.vmap(lambda one_key: jax.random.permutation(one_key, NKB)[:LIST])(row_keys[:NQB])
    counts = jax.random.randint(row_keys[NQB], (NQB,), 1, LIST + 1)
    fullest = jax.random.randint(row_keys[NQB + 1], (), 0, NQB)
    counts = jnp.where(jnp.arange(NQB) == fullest, LIST, counts)
    return jnp.where(jnp.arange(LIST)[None, :] < counts[:, None], picked, -1).astype(jnp.int32)


def draw_bin_edges(key, part):
    inner = jax.random.permutation(jax.random.fold_in(key, 404), S - 1)[:NBINS - 1] + 1
    inner = jnp.sort(inner)
    return jnp.concatenate([jnp.zeros((1,), jnp.int32), inner.astype(jnp.int32), jnp.full((1,), S, jnp.int32)])


def setup_inputs(seed: int = 0, part: int = 0) -> dict:
    splits = jax.random.split(jax.random.key(seed), 6)
    part_keys = jax.random.split(jax.random.fold_in(splits[5], part), 6)
    return {
        "queries": draw_queries(jax.random.fold_in(jax.random.fold_in(splits[5], part), 71), part),
        "key_states": draw_key_states(jax.random.fold_in(jax.random.fold_in(splits[5], part), 71), part),
        "obs_positions": draw_obs_positions(jax.random.fold_in(jax.random.fold_in(splits[5], part), 71), part),
        "block_lists": draw_block_lists(jax.random.fold_in(jax.random.fold_in(splits[5], part), 71), part),
        "bin_edges": draw_bin_edges(jax.random.fold_in(jax.random.fold_in(splits[5], part), 71), part),
    }


NEG = -1.0e30


def reference(queries, key_states, obs_positions, block_lists, bin_edges):
    scale = HD ** -0.5
    query_blocks = queries.astype(jnp.float32).reshape(NQB, OBS_DEV, KVH, QPK, HD)
    key_heads = jnp.moveaxis(key_states.astype(jnp.float32), 1, 0)
    position_blocks = obs_positions.reshape(NQB, OBS_DEV)
    key_pos = jnp.arange(S, dtype=jnp.int32)
    key_block = key_pos // KB

    def one_block(triple):
        query_block, positions, listed_ids = triple
        listed = jnp.any(listed_ids[:, None] == key_block[None, :], axis=0)
        own_block = key_block[None, :] == (positions // KB)[:, None]
        causal = key_pos[None, :] <= positions[:, None]
        masked = (causal & (listed[None, :] | own_block))[:, None, :]

        def one_group(pair):
            query_group, key_group = pair
            scores = jnp.einsum("pqd,nd->pqn", query_group, key_group, precision=lax.Precision.HIGHEST) * scale
            peak = jnp.max(jnp.where(masked, scores, NEG), axis=-1, keepdims=True)
            summed = jnp.sum(jnp.where(masked, jnp.exp(scores - peak), 0.0), axis=-1, keepdims=True)
            log_total = peak + jnp.log(summed)
            weight = jnp.where(masked, jnp.exp(scores - log_total), 0.0)
            return jnp.sum(weight, axis=(0, 1))

        return lax.map(one_group, (jnp.moveaxis(query_block, 1, 0), key_heads))

    partials = lax.map(one_block, (query_blocks, position_blocks, block_lists))
    key_mass = jnp.sum(partials, axis=0) * (S / (OBS * QPK))
    member = ((key_pos[:, None] >= bin_edges[None, :-1]) & (key_pos[:, None] < bin_edges[None, 1:])).astype(jnp.float32)
    widths = (bin_edges[1:] - bin_edges[:-1]).astype(jnp.float32)
    bin_sums = jnp.dot(key_mass, member, precision=lax.Precision.HIGHEST, preferred_element_type=jnp.float32)
    bin_density = bin_sums / widths[None, :]
    return key_mass, bin_density
```

```python
import math

import jax
import jax.numpy as jnp
from jax import lax
from jax.experimental import pallas as pl
from jax.experimental.pallas import tpu as pltpu
from jax.sharding import PartitionSpec as P

KB = 64
NEG = -1e30
LOG2E = math.log2(math.e)
VMEM = pl.BlockSpec(memory_space=pltpu.VMEM)


def xor_pairs(count, distance):
    return [(i, i ^ distance) for i in range(count)]


def visible_bias(positions, lists, owners, local_keys):
    rows = positions.shape[0]
    per_list = rows // lists.shape[0]
    key_pos = (owners[:, None] * local_keys + jnp.arange(local_keys, dtype=jnp.int32)).reshape(-1)
    key_block = key_pos // KB
    listed = jnp.any(lists[:, :, None] == key_block[None, None, :], axis=1)
    listed = jnp.broadcast_to(listed[:, None, :], (lists.shape[0], per_list, key_pos.shape[0]))
    listed = listed.reshape(rows, -1)
    own_block = key_block[None, :] == (positions // KB)[:, None]
    seen = (key_pos[None, :] <= positions[:, None]) & (listed | own_block)
    return jnp.where(seen, 0.0, NEG).astype(jnp.float32)


def mass_call(own_queries, sibling_queries, keys, bias, scale, factor):
    half, _, per_group, head_dim = own_queries.shape
    chunks = len(keys)
    groups, local_keys, _ = keys[0].shape
    total = chunks * local_keys
    step = max(8, min(half, (1 << 20) // (per_group * total)))

    def kernel(own_ref, sibling_ref, *refs):
        key_refs, bias_ref, out_ref, all_keys = refs[:chunks], refs[chunks], refs[-2], refs[-1]
        sub = lax.axis_index("sub")
        ctx = lax.axis_index("ctx")
        for index, key_ref in enumerate(key_refs):
            all_keys[:, index * local_keys : (index + 1) * local_keys, :] = key_ref[...]
        for group in range(groups):
            block_keys = all_keys[group]
            mass = jnp.zeros((per_group, total), jnp.float32)
            for part, query_ref in enumerate((own_ref, sibling_ref)):

                def advance(index, mass):
                    rows = query_ref[pl.ds(index * step, step), sub * groups + group]
                    scores = lax.dot_general(
                        rows.reshape(step * per_group, head_dim),
                        block_keys,
                        (((1,), (1,)), ((), ())),
                        preferred_element_type=jnp.float32,
                    ).reshape(step, per_group, total)
                    hidden = bias_ref[pl.ds(part * half + index * step, step), :]
                    scores = scores + hidden[:, None, :]
                    peak = jnp.max(scores, axis=-1, keepdims=True)
                    terms = jnp.exp2((scores - peak) * (scale * LOG2E))
                    weight = 1.0 / jnp.sum(terms, axis=-1, keepdims=True)
                    return mass + jnp.sum(terms * weight, axis=0)

                if step == half:
                    mass = advance(0, mass)
                else:
                    mass = lax.fori_loop(0, half // step, advance, mass)
            row = jnp.sum(mass, axis=0, keepdims=True) * factor
            for index in range(chunks):
                owner = jnp.bitwise_xor(ctx, index)
                out_ref[pl.ds(group * chunks + owner, 1), :] = row[
                    :, index * local_keys : (index + 1) * local_keys
                ]

    return pl.pallas_call(
        kernel,
        out_shape=jax.ShapeDtypeStruct((groups * chunks, local_keys), jnp.float32),
        in_specs=[VMEM] * (3 + chunks),
        out_specs=VMEM,
        scratch_shapes=[pltpu.VMEM((groups, total, head_dim), jnp.bfloat16)],
        compiler_params=pltpu.CompilerParams(vmem_limit_bytes=32 << 20),
        cost_estimate=pl.CostEstimate(
            flops=4 * half * per_group * groups * total * head_dim,
            bytes_accessed=1 << 20,
            transcendentals=2 * half * per_group * groups * total,
        ),
    )(own_queries, sibling_queries, *keys, bias)


def finish_call(mine, theirs, edges, groups, chunks):
    rows, local_keys = mine.shape
    half = rows // 2
    bins = edges.shape[1]

    def kernel(mine_ref, theirs_ref, edges_ref, mass_ref, bins_ref, total):
        sub = lax.axis_index("sub")
        ctx = lax.axis_index("ctx")
        for part in range(2):
            place = jnp.bitwise_xor(sub, part) * half
            rows_here = slice(part * half, (part + 1) * half)
            total[pl.ds(place, half), :] = mine_ref[rows_here, :] + theirs_ref[rows_here, :]
        low, high = edges_ref[0:1, :], edges_ref[1:2, :]
        sums = jnp.zeros((2 * groups * 3, bins), jnp.float32)
        for chunk in range(chunks):
            values = jnp.concatenate(
                [total[group * chunks + chunk][None, :] for group in range(2 * groups)], axis=0
            )
            first = values.astype(jnp.bfloat16)
            rest = values - first.astype(jnp.float32)
            second = rest.astype(jnp.bfloat16)
            third = (rest - second.astype(jnp.float32)).astype(jnp.bfloat16)
            split = jnp.concatenate([first, second, third], axis=0)
            key_pos = chunk * local_keys + lax.broadcasted_iota(jnp.int32, (local_keys, bins), 0)
            member = jnp.where((key_pos >= low) & (key_pos < high), 1.0, 0.0).astype(jnp.bfloat16)
            sums = sums + jnp.dot(split, member, preferred_element_type=jnp.float32)
        count = 2 * groups
        summed = sums[:count] + sums[count : 2 * count] + sums[2 * count :]
        bins_ref[...] = summed / (high - low).astype(jnp.float32)
        for group in range(2 * groups):
            mass_ref[group : group + 1, :] = total[pl.ds(group * chunks + ctx, 1), :]

    return pl.pallas_call(
        kernel,
        out_shape=(
            jax.ShapeDtypeStruct((2 * groups, local_keys), jnp.float32),
            jax.ShapeDtypeStruct((2 * groups, bins), jnp.float32),
        ),
        in_specs=[VMEM] * 3,
        out_specs=(VMEM, VMEM),
        scratch_shapes=[pltpu.VMEM((rows, local_keys), jnp.float32)],
        compiler_params=pltpu.CompilerParams(vmem_limit_bytes=4 << 20),
    )(mine, theirs, edges)


def local(queries, key_states, obs_positions, block_lists, bin_edges):
    query_rows, heads_dev, head_dim = queries.shape
    local_keys, groups_dev, _ = key_states.shape
    per_group = heads_dev // groups_dev
    ctx_count = lax.axis_size("ctx")
    sub_count = lax.axis_size("sub")
    both_count = ctx_count * sub_count
    groups = groups_dev // sub_count
    sub = lax.axis_index("sub")
    ctx = lax.axis_index("ctx")
    scale = head_dim ** (-0.5)
    factor = ctx_count * local_keys / (query_rows * both_count * per_group)

    own_keys = lax.dynamic_slice_in_dim(key_states, sub * groups, groups, 1)
    own_keys = jnp.transpose(own_keys, (1, 0, 2))
    keys = [own_keys] + [
        lax.ppermute(own_keys, "ctx", xor_pairs(ctx_count, distance))
        for distance in range(1, ctx_count)
    ]

    swap = xor_pairs(sub_count, 1)
    queries4 = queries.reshape(query_rows, groups_dev, per_group, head_dim)
    sibling_queries = lax.ppermute(queries4, "sub", swap)
    facts = jnp.concatenate([obs_positions, block_lists.reshape(-1)])
    sibling_facts = lax.ppermute(facts, "sub", swap)
    both_facts = jnp.stack([facts, sibling_facts])
    owners = jnp.bitwise_xor(ctx, jnp.arange(ctx_count, dtype=jnp.int32))
    bias = visible_bias(
        both_facts[:, :query_rows].reshape(-1), both_facts[:, query_rows:], owners, local_keys
    )

    mass = mass_call(queries4, sibling_queries, keys, bias, scale, factor)

    near = lax.ppermute(mass, "ctx", xor_pairs(ctx_count, 1))
    aside = lax.ppermute(mass, "sub", swap)
    across = lax.ppermute(mass, ("ctx", "sub"), xor_pairs(both_count, 3))
    mine = jnp.concatenate([mass + near, aside + across])
    theirs = None
    distance = 2
    while distance < ctx_count:
        if theirs is not None:
            mine = mine + theirs
        theirs = lax.ppermute(mine, "ctx", xor_pairs(ctx_count, distance))
        distance *= 2
    edges = jnp.stack([bin_edges[:-1], bin_edges[1:]])
    return finish_call(mine, theirs, edges, groups, ctx_count)


def solution(mesh):
    return jax.shard_map(
        local,
        mesh=mesh,
        in_specs=(
            P(("groups", "ctx", "sub"), "kvh", None),
            P(("groups", "ctx"), "kvh", None),
            P(("groups", "ctx", "sub")),
            P(("groups", "ctx", "sub"), None),
            P("groups"),
        ),
        out_specs=(P("kvh", ("groups", "ctx")), P("kvh", "groups")),
        check_vma=False,
    )
```

```python
import math

import jax
import jax.numpy as jnp
from jax import lax
from jax.experimental import pallas as pl
from jax.experimental.pallas import tpu as pltpu
from jax.sharding import PartitionSpec as P


KB = 64
NEG = -1e30
LOG2E = math.log2(math.e)
VMEM = pl.BlockSpec(memory_space=pltpu.VMEM)


def xor_pairs(count, distance):
    return [(i, i ^ distance) for i in range(count)]


def visible_bias(positions, lists, owners, local_keys):
    rows = positions.shape[0]
    per_list = rows // lists.shape[0]
    key_pos = (owners[:, None] * local_keys + jnp.arange(local_keys, dtype=jnp.int32)).reshape(-1)
    key_block = key_pos // KB
    listed = jnp.any(lists[:, :, None] == key_block[None, None, :], axis=1)
    listed = jnp.broadcast_to(listed[:, None, :], (lists.shape[0], per_list, key_pos.shape[0]))
    listed = listed.reshape(rows, -1)
    own_block = key_block[None, :] == (positions // KB)[:, None]
    seen = (key_pos[None, :] <= positions[:, None]) & (listed | own_block)
    return jnp.where(seen, 0.0, NEG).astype(jnp.float32)


def mass_call(own_queries, sibling_queries, keys, order, bias, scale, factor):
    half, _, per_group, head_dim = own_queries.shape
    chunks = len(keys)
    groups, local_keys, _ = keys[0].shape
    total = chunks * local_keys
    step = max(8, min(half, (1 << 20) // (per_group * total)))

    def kernel(own_ref, sibling_ref, *refs):
        key_refs, bias_ref, out_ref, all_keys = refs[:chunks], refs[chunks], refs[-2], refs[-1]
        sub = lax.axis_index("sub")
        ctx = lax.axis_index("ctx")
        for index, key_ref in enumerate(key_refs):
            all_keys[:, index * local_keys : (index + 1) * local_keys, :] = key_ref[...]
        for group in range(groups):
            block_keys = all_keys[group]
            mass = jnp.zeros((per_group, total), jnp.float32)
            for part, query_ref in enumerate((own_ref, sibling_ref)):

                def advance(index, mass):
                    rows = query_ref[pl.ds(index * step, step), part * (sub * groups) + group]
                    scores = lax.dot_general(
                        rows.reshape(step * per_group, head_dim),
                        block_keys,
                        (((1,), (1,)), ((), ())),
                        preferred_element_type=jnp.float32,
                    ).reshape(step, per_group, total)
                    hidden = bias_ref[pl.ds(part * half + index * step, step), :]
                    scores = scores + hidden[:, None, :]
                    peak = jnp.max(scores, axis=-1, keepdims=True)
                    terms = jnp.exp2((scores - peak) * (scale * LOG2E))
                    weight = 1.0 / jnp.sum(terms, axis=-1, keepdims=True)
                    return mass + jnp.sum(terms * weight, axis=0)

                if step == half:
                    mass = advance(0, mass)
                else:
                    mass = lax.fori_loop(0, half // step, advance, mass)
            row = jnp.sum(mass, axis=0, keepdims=True) * factor
            for index in range(chunks):
                owner = jnp.bitwise_xor(ctx, (0, *order)[index])
                out_ref[pl.ds(group * chunks + owner, 1), :] = row[
                    :, index * local_keys : (index + 1) * local_keys
                ]

    return pl.pallas_call(
        kernel,
        out_shape=jax.ShapeDtypeStruct((groups * chunks, local_keys), jnp.float32),
        in_specs=[VMEM] * (3 + chunks),
        out_specs=VMEM,
        scratch_shapes=[pltpu.VMEM((groups, total, head_dim), jnp.bfloat16)],
        compiler_params=pltpu.CompilerParams(vmem_limit_bytes=32 << 20),
        cost_estimate=pl.CostEstimate(
            flops=4 * half * per_group * groups * total * head_dim,
            bytes_accessed=1 << 20,
            transcendentals=2 * half * per_group * groups * total,
        ),
    )(own_queries, sibling_queries, *keys, bias)


def finish_call(mine, theirs, edges, groups, chunks):
    rows, local_keys = mine.shape
    half = rows // 2
    bins = edges.shape[1]

    def kernel(mine_ref, theirs_ref, edges_ref, mass_ref, bins_ref, total):
        sub = lax.axis_index("sub")
        ctx = lax.axis_index("ctx")
        for part in range(2):
            place = jnp.bitwise_xor(sub, part) * half
            rows_here = slice(part * half, (part + 1) * half)
            total[pl.ds(place, half), :] = mine_ref[rows_here, :] + theirs_ref[rows_here, :]
        low, high = edges_ref[0:1, :], edges_ref[1:2, :]
        sums = jnp.zeros((2 * groups * 3, bins), jnp.float32)
        for chunk in range(chunks):
            values = jnp.concatenate(
                [total[group * chunks + chunk][None, :] for group in range(2 * groups)], axis=0
            )
            first = values.astype(jnp.bfloat16)
            rest = values - first.astype(jnp.float32)
            second = rest.astype(jnp.bfloat16)
            third = (rest - second.astype(jnp.float32)).astype(jnp.bfloat16)
            split = jnp.concatenate([first, second, third], axis=0)
            key_pos = chunk * local_keys + lax.broadcasted_iota(jnp.int32, (local_keys, bins), 0)
            member = jnp.where((key_pos >= low) & (key_pos < high), 1.0, 0.0).astype(jnp.bfloat16)
            sums = sums + jnp.dot(split, member, preferred_element_type=jnp.float32)
        count = 2 * groups
        summed = sums[:count] + sums[count : 2 * count] + sums[2 * count :]
        bins_ref[...] = summed / (high - low).astype(jnp.float32)
        for group in range(2 * groups):
            mass_ref[group : group + 1, :] = total[pl.ds(group * chunks + ctx, 1), :]

    return pl.pallas_call(
        kernel,
        out_shape=(
            jax.ShapeDtypeStruct((2 * groups, local_keys), jnp.float32),
            jax.ShapeDtypeStruct((2 * groups, bins), jnp.float32),
        ),
        in_specs=[VMEM] * 3,
        out_specs=(VMEM, VMEM),
        scratch_shapes=[pltpu.VMEM((rows, local_keys), jnp.float32)],
        compiler_params=pltpu.CompilerParams(vmem_limit_bytes=4 << 20),
    )(mine, theirs, edges)


def local(queries, key_states, obs_positions, block_lists, bin_edges):
    query_rows, heads_dev, head_dim = queries.shape
    local_keys, groups_dev, _ = key_states.shape
    per_group = heads_dev // groups_dev
    ctx_count = lax.axis_size("ctx")
    sub_count = lax.axis_size("sub")
    both_count = ctx_count * sub_count
    groups = groups_dev // sub_count
    sub = lax.axis_index("sub")
    ctx = lax.axis_index("ctx")
    scale = head_dim ** (-0.5)
    factor = ctx_count * local_keys / (query_rows * both_count * per_group)

    order = [2, 3, 1] if ctx_count == 4 else list(range(1, ctx_count))
    own_keys = lax.dynamic_slice_in_dim(key_states, sub * groups, groups, 1)
    own_keys = jnp.transpose(own_keys, (1, 0, 2))
    keys = [own_keys] + [
        lax.ppermute(own_keys, "ctx", xor_pairs(ctx_count, distance))
        for distance in order
    ]

    swap = xor_pairs(sub_count, 1)
    queries4 = queries.reshape(query_rows, groups_dev, per_group, head_dim)
    sibling_queries = lax.ppermute(queries4, "sub", swap)
    positions = jnp.concatenate([obs_positions, lax.ppermute(obs_positions, "sub", swap)])
    lists = jnp.concatenate([block_lists, lax.ppermute(block_lists, "sub", swap)])
    owners = jnp.bitwise_xor(ctx, jnp.array([0, *order], jnp.int32))
    bias = visible_bias(positions, lists, owners, local_keys)

    own_queries = lax.dynamic_slice_in_dim(queries4, sub * groups, groups, 1)
    mass = mass_call(own_queries, sibling_queries, keys, order, bias, scale, factor)

    near = lax.ppermute(mass, "ctx", xor_pairs(ctx_count, 1))
    aside = lax.ppermute(mass, "sub", swap)
    across = lax.ppermute(mass, ("ctx", "sub"), xor_pairs(both_count, 3))
    mine = jnp.concatenate([mass + near, aside + across])
    theirs = None
    distance = 2
    while distance < ctx_count:
        if theirs is not None:
            mine = mine + theirs
        theirs = lax.ppermute(mine, "ctx", xor_pairs(ctx_count, distance))
        distance *= 2
    edges = jnp.stack([bin_edges[:-1], bin_edges[1:]])
    return finish_call(mine, theirs, edges, groups, ctx_count)


def solution(mesh):
    return jax.shard_map(
        local,
        mesh=mesh,
        in_specs=(
            P(("groups", "ctx", "sub"), "kvh", None),
            P(("groups", "ctx"), "kvh", None),
            P(("groups", "ctx", "sub")),
            P(("groups", "ctx", "sub"), None),
            P("groups"),
        ),
        out_specs=(P("kvh", ("groups", "ctx")), P("kvh", "groups")),
        check_vma=False,
    )
```

```python
import math

import jax
import jax.numpy as jnp
from jax import lax
from jax.experimental import pallas as pl
from jax.experimental.pallas import tpu as pltpu
from jax.sharding import PartitionSpec as P


KB = 64
NEG = -1e30
LOG2E = math.log2(math.e)
VMEM = pl.BlockSpec(memory_space=pltpu.VMEM)


def xor_pairs(count, distance):
    return [(i, i ^ distance) for i in range(count)]


def visible_bias(positions, lists, owners, local_keys):
    rows = positions.shape[0]
    per_list = rows // lists.shape[0]
    key_pos = (owners[:, None] * local_keys + jnp.arange(local_keys, dtype=jnp.int32)).reshape(-1)
    key_block = key_pos // KB
    listed = jnp.any(lists[:, :, None] == key_block[None, None, :], axis=1)
    listed = jnp.broadcast_to(listed[:, None, :], (lists.shape[0], per_list, key_pos.shape[0]))
    listed = listed.reshape(rows, -1)
    own_block = key_block[None, :] == (positions // KB)[:, None]
    seen = (key_pos[None, :] <= positions[:, None]) & (listed | own_block)
    return jnp.where(seen, 0.0, NEG).astype(jnp.float32)


def mass_call(own_queries, sibling_queries, keys, order, bias, scale, factor):
    half, _, per_group, head_dim = own_queries.shape
    chunks = len(keys)
    groups, local_keys, _ = keys[0].shape
    total = chunks * local_keys
    step = max(8, min(half, (1 << 20) // (per_group * total)))

    def kernel(own_ref, sibling_ref, *refs):
        key_refs, bias_ref, out_ref, all_keys = refs[:chunks], refs[chunks], refs[-2], refs[-1]
        sub = lax.axis_index("sub")
        ctx = lax.axis_index("ctx")
        for index, key_ref in enumerate(key_refs):
            all_keys[:, index * local_keys : (index + 1) * local_keys, :] = key_ref[...]
        for group in range(groups):
            block_keys = all_keys[group]
            mass = jnp.zeros((per_group, total), jnp.float32)
            for part, query_ref in enumerate((own_ref, sibling_ref)):

                def advance(index, mass):
                    rows = query_ref[pl.ds(index * step, step), part * (sub * groups) + group]
                    scores = lax.dot_general(
                        rows.reshape(step * per_group, head_dim),
                        block_keys,
                        (((1,), (1,)), ((), ())),
                        preferred_element_type=jnp.float32,
                    ).reshape(step, per_group, total)
                    first = part * half + index * step
                    if isinstance(first, int):
                        spread = [
                            bias_ref[pl.ds(first + row, per_group, stride=0), :]
                            for row in range(step)
                        ]
                        hidden = jnp.stack(spread)
                    else:
                        hidden = bias_ref[pl.ds(first, step), :][:, None, :]
                    scores = scores + hidden
                    peak = jnp.max(scores, axis=-1, keepdims=True)
                    terms = jnp.exp2((scores - peak) * (scale * LOG2E))
                    weight = 1.0 / jnp.sum(terms, axis=-1, keepdims=True)
                    return mass + jnp.sum(terms * weight, axis=0)

                if step == half:
                    mass = advance(0, mass)
                else:
                    mass = lax.fori_loop(0, half // step, advance, mass)
            row = jnp.sum(mass, axis=0, keepdims=True) * factor
            for index in range(chunks):
                owner = jnp.bitwise_xor(ctx, (0, *order)[index])
                out_ref[pl.ds(group * chunks + owner, 1), :] = row[
                    :, index * local_keys : (index + 1) * local_keys
                ]

    return pl.pallas_call(
        kernel,
        out_shape=jax.ShapeDtypeStruct((groups * chunks, local_keys), jnp.float32),
        in_specs=[VMEM] * (3 + chunks),
        out_specs=VMEM,
        scratch_shapes=[pltpu.VMEM((groups, total, head_dim), jnp.bfloat16)],
        compiler_params=pltpu.CompilerParams(vmem_limit_bytes=32 << 20),
        cost_estimate=pl.CostEstimate(
            flops=4 * half * per_group * groups * total * head_dim,
            bytes_accessed=1 << 20,
            transcendentals=2 * half * per_group * groups * total,
        ),
    )(own_queries, sibling_queries, *keys, bias)


def finish_call(mine, theirs, edges, groups, chunks):
    rows, local_keys = mine.shape
    half = rows // 2
    bins = edges.shape[1]

    def kernel(mine_ref, theirs_ref, edges_ref, mass_ref, bins_ref, total):
        sub = lax.axis_index("sub")
        ctx = lax.axis_index("ctx")
        for part in range(2):
            place = jnp.bitwise_xor(sub, part) * half
            rows_here = slice(part * half, (part + 1) * half)
            total[pl.ds(place, half), :] = mine_ref[rows_here, :] + theirs_ref[rows_here, :]
        low, high = edges_ref[0:1, :], edges_ref[1:2, :]
        sums = jnp.zeros((2 * groups * 3, bins), jnp.float32)
        for chunk in range(chunks):
            values = jnp.concatenate(
                [total[group * chunks + chunk][None, :] for group in range(2 * groups)], axis=0
            )
            first = values.astype(jnp.bfloat16)
            rest = values - first.astype(jnp.float32)
            second = rest.astype(jnp.bfloat16)
            third = (rest - second.astype(jnp.float32)).astype(jnp.bfloat16)
            split = jnp.concatenate([first, second, third], axis=0)
            key_pos = chunk * local_keys + lax.broadcasted_iota(jnp.int32, (local_keys, bins), 0)
            member = jnp.where((key_pos >= low) & (key_pos < high), 1.0, 0.0).astype(jnp.bfloat16)
            sums = sums + jnp.dot(split, member, preferred_element_type=jnp.float32)
        count = 2 * groups
        summed = sums[:count] + sums[count : 2 * count] + sums[2 * count :]
        bins_ref[...] = summed / (high - low).astype(jnp.float32)
        for group in range(2 * groups):
            mass_ref[group : group + 1, :] = total[pl.ds(group * chunks + ctx, 1), :]

    return pl.pallas_call(
        kernel,
        out_shape=(
            jax.ShapeDtypeStruct((2 * groups, local_keys), jnp.float32),
            jax.ShapeDtypeStruct((2 * groups, bins), jnp.float32),
        ),
        in_specs=[VMEM] * 3,
        out_specs=(VMEM, VMEM),
        scratch_shapes=[pltpu.VMEM((rows, local_keys), jnp.float32)],
        compiler_params=pltpu.CompilerParams(vmem_limit_bytes=4 << 20),
    )(mine, theirs, edges)


def local(queries, key_states, obs_positions, block_lists, bin_edges):
    query_rows, heads_dev, head_dim = queries.shape
    local_keys, groups_dev, _ = key_states.shape
    per_group = heads_dev // groups_dev
    ctx_count = lax.axis_size("ctx")
    sub_count = lax.axis_size("sub")
    both_count = ctx_count * sub_count
    groups = groups_dev // sub_count
    sub = lax.axis_index("sub")
    ctx = lax.axis_index("ctx")
    scale = head_dim ** (-0.5)
    factor = ctx_count * local_keys / (query_rows * both_count * per_group)

    order = [2, 3, 1] if ctx_count == 4 else list(range(1, ctx_count))
    own_keys = lax.dynamic_slice_in_dim(key_states, sub * groups, groups, 1)
    own_keys = jnp.transpose(own_keys, (1, 0, 2))
    keys = [own_keys] + [
        lax.ppermute(own_keys, "ctx", xor_pairs(ctx_count, distance))
        for distance in order
    ]

    swap = xor_pairs(sub_count, 1)
    queries4 = queries.reshape(query_rows, groups_dev, per_group, head_dim)
    sibling_queries = lax.ppermute(queries4, "sub", swap)
    positions = jnp.concatenate([obs_positions, lax.ppermute(obs_positions, "sub", swap)])
    lists = jnp.concatenate([block_lists, lax.ppermute(block_lists, "sub", swap)])
    owners = jnp.bitwise_xor(ctx, jnp.array([0, *order], jnp.int32))
    bias = visible_bias(positions, lists, owners, local_keys)

    own_queries = lax.dynamic_slice_in_dim(queries4, sub * groups, groups, 1)
    mass = mass_call(own_queries, sibling_queries, keys, order, bias, scale, factor)

    near = lax.ppermute(mass, "ctx", xor_pairs(ctx_count, 1))
    aside = lax.ppermute(mass, "sub", swap)
    across = lax.ppermute(mass, ("ctx", "sub"), xor_pairs(both_count, 3))
    mine = jnp.concatenate([mass + near, aside + across])
    theirs = None
    distance = 2
    while distance < ctx_count:
        if theirs is not None:
            mine = mine + theirs
        theirs = lax.ppermute(mine, "ctx", xor_pairs(ctx_count, distance))
        distance *= 2
    edges = jnp.stack([bin_edges[:-1], bin_edges[1:]])
    return finish_call(mine, theirs, edges, groups, ctx_count)


def solution(mesh):
    return jax.shard_map(
        local,
        mesh=mesh,
        in_specs=(
            P(("groups", "ctx", "sub"), "kvh", None),
            P(("groups", "ctx"), "kvh", None),
            P(("groups", "ctx", "sub")),
            P(("groups", "ctx", "sub"), None),
            P("groups"),
        ),
        out_specs=(P("kvh", ("groups", "ctx")), P("kvh", "groups")),
        check_vma=False,
    )
```

```python
import math

import jax
import jax.numpy as jnp
from jax import lax
from jax.experimental import pallas as pl
from jax.experimental.pallas import tpu as pltpu
from jax.sharding import PartitionSpec as P


KB = 64
NEG = -1e30
LOG2E = math.log2(math.e)
VMEM = pl.BlockSpec(memory_space=pltpu.VMEM)


def xor_pairs(count, distance):
    return [(i, i ^ distance) for i in range(count)]


def visible_bias(positions, lists, owners, local_keys):
    rows = positions.shape[0]
    per_list = rows // lists.shape[0]
    key_pos = (owners[:, None] * local_keys + jnp.arange(local_keys, dtype=jnp.int32)).reshape(-1)
    key_block = key_pos // KB
    listed = jnp.any(lists[:, :, None] == key_block[None, None, :], axis=1)
    listed = jnp.broadcast_to(listed[:, None, :], (lists.shape[0], per_list, key_pos.shape[0]))
    listed = listed.reshape(rows, -1)
    own_block = key_block[None, :] == (positions // KB)[:, None]
    seen = (key_pos[None, :] <= positions[:, None]) & (listed | own_block)
    return jnp.where(seen, 0.0, NEG).astype(jnp.float32)


def scaled_parts(values, scale):
    scaled = values.astype(jnp.float32) * scale
    upper = lax.reduce_precision(scaled, exponent_bits=8, mantissa_bits=7)
    return [upper.astype(jnp.bfloat16), (scaled - upper).astype(jnp.bfloat16)]


def mass_call(query_parts, keys, order, bias, factor):
    half, _, per_group, head_dim = query_parts[0].shape
    chunks = len(keys)
    groups, local_keys, _ = keys[0].shape
    total = chunks * local_keys
    step = max(8, min(half, (1 << 20) // (per_group * total)))

    def kernel(*refs):
        query_refs, refs = refs[:4], refs[4:]
        key_refs, bias_ref, out_ref = refs[:chunks], refs[chunks], refs[-1]
        ctx = lax.axis_index("ctx")
        for group in range(groups):
            block_keys = jnp.concatenate([key_ref[group] for key_ref in key_refs], axis=0)
            block_keys = jnp.concatenate([block_keys, block_keys], axis=1)
            mass = jnp.zeros((per_group, total), jnp.float32)
            for part in range(2):

                def advance(index, mass):
                    rows = [
                        query_ref[pl.ds(index * step, step), group].reshape(-1, head_dim)
                        for query_ref in query_refs[2 * part : 2 * part + 2]
                    ]
                    scores = lax.dot_general(
                        jnp.concatenate(rows, axis=1),
                        block_keys,
                        (((1,), (1,)), ((), ())),
                        preferred_element_type=jnp.float32,
                    ).reshape(step, per_group, total)
                    first = part * half + index * step
                    if isinstance(first, int):
                        spread = [
                            bias_ref[pl.ds(first + row, per_group, stride=0), :]
                            for row in range(step)
                        ]
                        hidden = jnp.stack(spread)
                    else:
                        hidden = bias_ref[pl.ds(first, step), :][:, None, :]
                    scores = scores + hidden
                    peak = jnp.max(scores, axis=-1, keepdims=True)
                    terms = jnp.exp2(scores - peak)
                    weight = 1.0 / jnp.sum(terms, axis=-1, keepdims=True)
                    return mass + jnp.sum(terms * weight, axis=0)

                if step == half:
                    mass = advance(0, mass)
                else:
                    mass = lax.fori_loop(0, half // step, advance, mass)
            row = jnp.sum(mass, axis=0, keepdims=True) * factor
            for index in range(chunks):
                owner = jnp.bitwise_xor(ctx, (0, *order)[index])
                out_ref[pl.ds(group * chunks + owner, 1), :] = row[
                    :, index * local_keys : (index + 1) * local_keys
                ]

    return pl.pallas_call(
        kernel,
        out_shape=jax.ShapeDtypeStruct((groups * chunks, local_keys), jnp.float32),
        in_specs=[VMEM] * (5 + chunks),
        out_specs=VMEM,
        compiler_params=pltpu.CompilerParams(vmem_limit_bytes=32 << 20),
        cost_estimate=pl.CostEstimate(
            flops=4 * half * per_group * groups * total * head_dim,
            bytes_accessed=1 << 20,
            transcendentals=2 * half * per_group * groups * total,
        ),
    )(*query_parts, *keys, bias)


def finish_call(mine, theirs, edges, groups, chunks):
    rows, local_keys = mine.shape
    half = rows // 2
    bins = edges.shape[1]

    def kernel(mine_ref, theirs_ref, edges_ref, mass_ref, bins_ref, total):
        sub = lax.axis_index("sub")
        ctx = lax.axis_index("ctx")
        for part in range(2):
            place = jnp.bitwise_xor(sub, part) * half
            rows_here = slice(part * half, (part + 1) * half)
            total[pl.ds(place, half), :] = mine_ref[rows_here, :] + theirs_ref[rows_here, :]
        low, high = edges_ref[0:1, :], edges_ref[1:2, :]
        sums = jnp.zeros((2 * groups * 3, bins), jnp.float32)
        for chunk in range(chunks):
            values = jnp.concatenate(
                [total[group * chunks + chunk][None, :] for group in range(2 * groups)], axis=0
            )
            first = values.astype(jnp.bfloat16)
            rest = values - first.astype(jnp.float32)
            second = rest.astype(jnp.bfloat16)
            third = (rest - second.astype(jnp.float32)).astype(jnp.bfloat16)
            split = jnp.concatenate([first, second, third], axis=0)
            key_pos = chunk * local_keys + lax.broadcasted_iota(jnp.int32, (local_keys, bins), 0)
            member = jnp.where((key_pos >= low) & (key_pos < high), 1.0, 0.0).astype(jnp.bfloat16)
            sums = sums + jnp.dot(split, member, preferred_element_type=jnp.float32)
        count = 2 * groups
        summed = sums[:count] + sums[count : 2 * count] + sums[2 * count :]
        bins_ref[...] = summed / (high - low).astype(jnp.float32)
        for group in range(2 * groups):
            mass_ref[group : group + 1, :] = total[pl.ds(group * chunks + ctx, 1), :]

    return pl.pallas_call(
        kernel,
        out_shape=(
            jax.ShapeDtypeStruct((2 * groups, local_keys), jnp.float32),
            jax.ShapeDtypeStruct((2 * groups, bins), jnp.float32),
        ),
        in_specs=[VMEM] * 3,
        out_specs=(VMEM, VMEM),
        scratch_shapes=[pltpu.VMEM((rows, local_keys), jnp.float32)],
        compiler_params=pltpu.CompilerParams(vmem_limit_bytes=4 << 20),
    )(mine, theirs, edges)


def local(queries, key_states, obs_positions, block_lists, bin_edges):
    query_rows, heads_dev, head_dim = queries.shape
    local_keys, groups_dev, _ = key_states.shape
    per_group = heads_dev // groups_dev
    ctx_count = lax.axis_size("ctx")
    sub_count = lax.axis_size("sub")
    both_count = ctx_count * sub_count
    groups = groups_dev // sub_count
    sub = lax.axis_index("sub")
    ctx = lax.axis_index("ctx")
    scale = head_dim ** (-0.5)
    factor = ctx_count * local_keys / (query_rows * both_count * per_group)

    order = [2, 3, 1] if ctx_count == 4 else list(range(1, ctx_count))
    own_keys = lax.dynamic_slice_in_dim(key_states, sub * groups, groups, 1)
    own_keys = jnp.transpose(own_keys, (1, 0, 2))
    keys = [own_keys] + [
        lax.ppermute(own_keys, "ctx", xor_pairs(ctx_count, distance))
        for distance in order
    ]

    swap = xor_pairs(sub_count, 1)
    queries4 = queries.reshape(query_rows, groups_dev, per_group, head_dim)
    sibling_queries = lax.ppermute(queries4, "sub", swap)
    positions = jnp.concatenate([obs_positions, lax.ppermute(obs_positions, "sub", swap)])
    lists = jnp.concatenate([block_lists, lax.ppermute(block_lists, "sub", swap)])
    owners = jnp.bitwise_xor(ctx, jnp.array([0, *order], jnp.int32))
    bias = visible_bias(positions, lists, owners, local_keys)

    query_parts = []
    for part in (queries4, sibling_queries):
        part = lax.dynamic_slice_in_dim(part, sub * groups, groups, 1)
        query_parts += scaled_parts(part, scale * LOG2E)
    mass = mass_call(query_parts, keys, order, bias, factor)

    near = lax.ppermute(mass, "ctx", xor_pairs(ctx_count, 1))
    aside = lax.ppermute(mass, "sub", swap)
    across = lax.ppermute(mass, ("ctx", "sub"), xor_pairs(both_count, 3))
    mine = jnp.concatenate([mass + near, aside + across])
    theirs = None
    distance = 2
    while distance < ctx_count:
        if theirs is not None:
            mine = mine + theirs
        theirs = lax.ppermute(mine, "ctx", xor_pairs(ctx_count, distance))
        distance *= 2
    edges = jnp.stack([bin_edges[:-1], bin_edges[1:]])
    return finish_call(mine, theirs, edges, groups, ctx_count)


def solution(mesh):
    return jax.shard_map(
        local,
        mesh=mesh,
        in_specs=(
            P(("groups", "ctx", "sub"), "kvh", None),
            P(("groups", "ctx"), "kvh", None),
            P(("groups", "ctx", "sub")),
            P(("groups", "ctx", "sub"), None),
            P("groups"),
        ),
        out_specs=(P("kvh", ("groups", "ctx")), P("kvh", "groups")),
        check_vma=False,
    )
```

```python
import math

import jax
import jax.numpy as jnp
from jax import lax
from jax.experimental import pallas as pl
from jax.experimental.pallas import tpu as pltpu
from jax.sharding import PartitionSpec as P


KB = 64
NEG = -1e30
LOG2E = math.log2(math.e)
VMEM = pl.BlockSpec(memory_space=pltpu.VMEM)


def xor_pairs(count, distance):
    return [(i, i ^ distance) for i in range(count)]


def visible_bias(positions, lists, owners, local_keys):
    rows = positions.shape[0]
    per_list = rows // lists.shape[0]
    key_pos = (owners[:, None] * local_keys + jnp.arange(local_keys, dtype=jnp.int32)).reshape(-1)
    key_block = key_pos // KB
    listed = jnp.any(lists[:, :, None] == key_block[None, None, :], axis=1)
    listed = jnp.broadcast_to(listed[:, None, :], (lists.shape[0], per_list, key_pos.shape[0]))
    listed = listed.reshape(rows, -1)
    own_block = key_block[None, :] == (positions // KB)[:, None]
    seen = (key_pos[None, :] <= positions[:, None]) & (listed | own_block)
    return jnp.where(seen, 0.0, NEG).astype(jnp.float32)


def scaled_parts(values, scale):
    scaled = values.astype(jnp.float32) * scale
    upper = lax.reduce_precision(scaled, exponent_bits=8, mantissa_bits=7)
    return [upper.astype(jnp.bfloat16), (scaled - upper).astype(jnp.bfloat16)]


def mass_call(query_parts, keys, order, bias, factor):
    half, _, per_group, head_dim = query_parts[0].shape
    chunks = len(keys)
    groups, local_keys, _ = keys[0].shape
    total = chunks * local_keys
    step = max(8, min(half, (1 << 20) // (per_group * total)))

    def kernel(*refs):
        query_refs, refs = refs[:4], refs[4:]
        key_refs, bias_ref, out_ref = refs[:chunks], refs[chunks], refs[-1]
        ctx = lax.axis_index("ctx")
        for group in range(groups):
            block_keys = jnp.concatenate([key_ref[group] for key_ref in key_refs], axis=0)
            block_keys = jnp.concatenate([block_keys, block_keys], axis=1)
            mass = jnp.zeros((per_group, total), jnp.float32)
            for part in range(2):

                def advance(index, mass):
                    rows = [
                        query_ref[pl.ds(index * step, step), group].reshape(-1, head_dim)
                        for query_ref in query_refs[2 * part : 2 * part + 2]
                    ]
                    scores = lax.dot_general(
                        jnp.concatenate(rows, axis=1),
                        block_keys,
                        (((1,), (1,)), ((), ())),
                        preferred_element_type=jnp.float32,
                    ).reshape(step, per_group, total)
                    first = part * half + index * step
                    if isinstance(first, int):
                        spread = [
                            bias_ref[pl.ds(first + row, per_group, stride=0), :]
                            for row in range(step)
                        ]
                        hidden = jnp.stack(spread)
                    else:
                        hidden = bias_ref[pl.ds(first, step), :][:, None, :]
                    scores = scores + hidden
                    peak = jnp.max(scores, axis=-1, keepdims=True)
                    terms = jnp.exp2(scores - peak)
                    weight = 1.0 / jnp.sum(terms, axis=-1, keepdims=True)
                    return mass + jnp.sum(terms * weight, axis=0)

                if step == half:
                    mass = advance(0, mass)
                else:
                    mass = lax.fori_loop(0, half // step, advance, mass)
            row = jnp.sum(mass, axis=0, keepdims=True) * factor
            for index in range(chunks):
                owner = jnp.bitwise_xor(ctx, (0, *order)[index])
                out_ref[pl.ds(group * chunks + owner, 1), :] = row[
                    :, index * local_keys : (index + 1) * local_keys
                ]

    return pl.pallas_call(
        kernel,
        out_shape=jax.ShapeDtypeStruct((groups * chunks, local_keys), jnp.float32),
        in_specs=[VMEM] * (5 + chunks),
        out_specs=VMEM,
        compiler_params=pltpu.CompilerParams(vmem_limit_bytes=32 << 20),
        cost_estimate=pl.CostEstimate(
            flops=4 * half * per_group * groups * total * head_dim,
            bytes_accessed=1 << 20,
            transcendentals=2 * half * per_group * groups * total,
        ),
    )(*query_parts, *keys, bias)


def finish_call(mine, theirs, edges, groups, chunks):
    rows, local_keys = mine.shape
    half = rows // 2
    bins = edges.shape[1]

    def kernel(mine_ref, theirs_ref, edges_ref, mass_ref, bins_ref, total):
        sub = lax.axis_index("sub")
        ctx = lax.axis_index("ctx")
        for part in range(2):
            place = jnp.bitwise_xor(sub, part) * half
            rows_here = slice(part * half, (part + 1) * half)
            swapped = slice((1 - part) * half, (2 - part) * half)
            total[pl.ds(place, half), :] = mine_ref[rows_here, :] + theirs_ref[swapped, :]
        low, high = edges_ref[0:1, :], edges_ref[1:2, :]
        sums = jnp.zeros((2 * groups * 3, bins), jnp.float32)
        for chunk in range(chunks):
            values = jnp.concatenate(
                [total[group * chunks + chunk][None, :] for group in range(2 * groups)], axis=0
            )
            first = values.astype(jnp.bfloat16)
            rest = values - first.astype(jnp.float32)
            second = rest.astype(jnp.bfloat16)
            third = (rest - second.astype(jnp.float32)).astype(jnp.bfloat16)
            split = jnp.concatenate([first, second, third], axis=0)
            key_pos = chunk * local_keys + lax.broadcasted_iota(jnp.int32, (local_keys, bins), 0)
            member = jnp.where((key_pos >= low) & (key_pos < high), 1.0, 0.0).astype(jnp.bfloat16)
            sums = sums + jnp.dot(split, member, preferred_element_type=jnp.float32)
        count = 2 * groups
        summed = sums[:count] + sums[count : 2 * count] + sums[2 * count :]
        bins_ref[...] = summed / (high - low).astype(jnp.float32)
        for group in range(2 * groups):
            mass_ref[group : group + 1, :] = total[pl.ds(group * chunks + ctx, 1), :]

    return pl.pallas_call(
        kernel,
        out_shape=(
            jax.ShapeDtypeStruct((2 * groups, local_keys), jnp.float32),
            jax.ShapeDtypeStruct((2 * groups, bins), jnp.float32),
        ),
        in_specs=[VMEM] * 3,
        out_specs=(VMEM, VMEM),
        scratch_shapes=[pltpu.VMEM((rows, local_keys), jnp.float32)],
        compiler_params=pltpu.CompilerParams(vmem_limit_bytes=4 << 20),
    )(mine, theirs, edges)


def local(queries, key_states, obs_positions, block_lists, bin_edges):
    query_rows, heads_dev, head_dim = queries.shape
    local_keys, groups_dev, _ = key_states.shape
    per_group = heads_dev // groups_dev
    ctx_count = lax.axis_size("ctx")
    sub_count = lax.axis_size("sub")
    both_count = ctx_count * sub_count
    groups = groups_dev // sub_count
    sub = lax.axis_index("sub")
    ctx = lax.axis_index("ctx")
    scale = head_dim ** (-0.5)
    factor = ctx_count * local_keys / (query_rows * both_count * per_group)

    order = [2, 3, 1] if ctx_count == 4 else list(range(1, ctx_count))
    own_keys = lax.dynamic_slice_in_dim(key_states, sub * groups, groups, 1)
    own_keys = jnp.transpose(own_keys, (1, 0, 2))
    keys = [own_keys] + [
        lax.ppermute(own_keys, "ctx", xor_pairs(ctx_count, distance))
        for distance in order
    ]

    swap = xor_pairs(sub_count, 1)
    queries4 = queries.reshape(query_rows, groups_dev, per_group, head_dim)
    sibling_queries = lax.ppermute(queries4, "sub", swap)
    positions = jnp.concatenate([obs_positions, lax.ppermute(obs_positions, "sub", swap)])
    lists = jnp.concatenate([block_lists, lax.ppermute(block_lists, "sub", swap)])
    owners = jnp.bitwise_xor(ctx, jnp.array([0, *order], jnp.int32))
    bias = visible_bias(positions, lists, owners, local_keys)

    query_parts = []
    for part in (queries4, sibling_queries):
        part = lax.dynamic_slice_in_dim(part, sub * groups, groups, 1)
        query_parts += scaled_parts(part, scale * LOG2E)
    mass = mass_call(query_parts, keys, order, bias, factor)

    near = lax.ppermute(mass, "ctx", xor_pairs(ctx_count, 1))
    aside = lax.ppermute(mass, "sub", swap)
    across = lax.ppermute(mass, ("ctx", "sub"), xor_pairs(both_count, 3))
    mine = jnp.concatenate([mass + near, aside + across])
    theirs = None
    distance = 2
    while distance < ctx_count:
        if theirs is not None:
            mine = mine + theirs
        last = distance * 2 >= ctx_count
        pairs = xor_pairs(both_count, distance * sub_count + (1 if last else 0))
        theirs = lax.ppermute(mine, ("ctx", "sub"), pairs)
        distance *= 2
    edges = jnp.stack([bin_edges[:-1], bin_edges[1:]])
    return finish_call(mine, theirs, edges, groups, ctx_count)


def solution(mesh):
    return jax.shard_map(
        local,
        mesh=mesh,
        in_specs=(
            P(("groups", "ctx", "sub"), "kvh", None),
            P(("groups", "ctx"), "kvh", None),
            P(("groups", "ctx", "sub")),
            P(("groups", "ctx", "sub"), None),
            P("groups"),
        ),
        out_specs=(P("kvh", ("groups", "ctx")), P("kvh", "groups")),
        check_vma=False,
    )
```

```python
import math

import jax
import jax.numpy as jnp
from jax import lax
from jax.experimental import pallas as pl
from jax.experimental.pallas import tpu as pltpu
from jax.sharding import PartitionSpec as P


KB = 64
NEG = -1e30
LOG2E = math.log2(math.e)
VMEM = pl.BlockSpec(memory_space=pltpu.VMEM)


def xor_pairs(count, distance):
    return [(i, i ^ distance) for i in range(count)]


def visible_bias(positions, lists, owners, local_keys):
    rows = positions.shape[0]
    per_list = rows // lists.shape[0]
    key_pos = (owners[:, None] * local_keys + jnp.arange(local_keys, dtype=jnp.int32)).reshape(-1)
    key_block = key_pos // KB
    listed = jnp.any(lists[:, :, None] == key_block[None, None, :], axis=1)
    listed = jnp.broadcast_to(listed[:, None, :], (lists.shape[0], per_list, key_pos.shape[0]))
    listed = listed.reshape(rows, -1)
    own_block = key_block[None, :] == (positions // KB)[:, None]
    seen = (key_pos[None, :] <= positions[:, None]) & (listed | own_block)
    return jnp.where(seen, 0.0, NEG).astype(jnp.float32)


def scaled_parts(values, scale):
    scaled = values.astype(jnp.float32) * scale
    upper = lax.reduce_precision(scaled, exponent_bits=8, mantissa_bits=7)
    return [upper.astype(jnp.bfloat16), (scaled - upper).astype(jnp.bfloat16)]


def mass_call(query_parts, keys, order, bias, factor):
    half, _, per_group, head_dim = query_parts[0].shape
    chunks = len(keys)
    groups, local_keys, _ = keys[0].shape
    total = chunks * local_keys
    step = max(8, min(half, (1 << 20) // (per_group * total)))

    def kernel(*refs):
        query_refs, refs = refs[:4], refs[4:]
        key_refs, bias_ref, out_ref = refs[:chunks], refs[chunks], refs[-1]
        ctx = lax.axis_index("ctx")
        for group in range(groups):
            block_keys = jnp.concatenate([key_ref[group] for key_ref in key_refs], axis=0)
            block_keys = jnp.concatenate([block_keys, block_keys], axis=1)
            mass = jnp.zeros((per_group, total), jnp.float32)
            for part in range(2):

                def advance(index, mass):
                    rows = [
                        query_ref[pl.ds(index * step, step), group].reshape(-1, head_dim)
                        for query_ref in query_refs[2 * part : 2 * part + 2]
                    ]
                    scores = lax.dot_general(
                        jnp.concatenate(rows, axis=1),
                        block_keys,
                        (((1,), (1,)), ((), ())),
                        preferred_element_type=jnp.float32,
                    ).reshape(step, per_group, total)
                    first = part * half + index * step
                    if isinstance(first, int):
                        spread = [
                            bias_ref[pl.ds(first + row, per_group, stride=0), :]
                            for row in range(step)
                        ]
                        hidden = jnp.stack(spread)
                    else:
                        hidden = bias_ref[pl.ds(first, step), :][:, None, :]
                    scores = scores + hidden
                    peak = jnp.max(scores, axis=-1, keepdims=True)
                    terms = jnp.exp2(scores - peak)
                    weight = 1.0 / jnp.sum(terms, axis=-1, keepdims=True)
                    return mass + jnp.sum(terms * weight, axis=0)

                if step == half:
                    mass = advance(0, mass)
                else:
                    mass = lax.fori_loop(0, half // step, advance, mass)
            row = jnp.sum(mass, axis=0, keepdims=True) * factor
            for index in range(chunks):
                owner = jnp.bitwise_xor(ctx, (0, *order)[index])
                out_ref[pl.ds(group * chunks + owner, 1), :] = row[
                    :, index * local_keys : (index + 1) * local_keys
                ]

    return pl.pallas_call(
        kernel,
        out_shape=jax.ShapeDtypeStruct((groups * chunks, local_keys), jnp.float32),
        in_specs=[VMEM] * (5 + chunks),
        out_specs=VMEM,
        compiler_params=pltpu.CompilerParams(vmem_limit_bytes=32 << 20),
        cost_estimate=pl.CostEstimate(
            flops=4 * half * per_group * groups * total * head_dim,
            bytes_accessed=1 << 20,
            transcendentals=2 * half * per_group * groups * total,
        ),
    )(*query_parts, *keys, bias)


def finish_call(mine, theirs, edges, groups, chunks):
    rows, local_keys = mine.shape
    half = rows // 2
    bins = edges.shape[1]

    def kernel(mine_ref, theirs_ref, edges_ref, mass_ref, bins_ref, total):
        sub = lax.axis_index("sub")
        ctx = lax.axis_index("ctx")
        for part in range(2):
            place = jnp.bitwise_xor(sub, part) * half
            rows_here = slice(part * half, (part + 1) * half)
            swapped = slice((1 - part) * half, (2 - part) * half)
            total[pl.ds(place, half), :] = mine_ref[rows_here, :] + theirs_ref[swapped, :]
        low, high = edges_ref[0:1, :], edges_ref[1:2, :]
        sums = jnp.zeros((2 * groups * 3, bins), jnp.float32)
        for chunk in range(chunks):
            values = jnp.concatenate(
                [total[group * chunks + chunk][None, :] for group in range(2 * groups)], axis=0
            )
            first = values.astype(jnp.bfloat16)
            rest = values - first.astype(jnp.float32)
            second = rest.astype(jnp.bfloat16)
            third = (rest - second.astype(jnp.float32)).astype(jnp.bfloat16)
            split = jnp.concatenate([first, second, third], axis=0)
            key_pos = chunk * local_keys + lax.broadcasted_iota(jnp.int32, (local_keys, bins), 0)
            member = jnp.where((key_pos >= low) & (key_pos < high), 1.0, 0.0).astype(jnp.bfloat16)
            sums = sums + jnp.dot(split, member, preferred_element_type=jnp.float32)
        count = 2 * groups
        summed = sums[:count] + sums[count : 2 * count] + sums[2 * count :]
        bins_ref[...] = summed / (high - low).astype(jnp.float32)
        for group in range(2 * groups):
            mass_ref[group : group + 1, :] = total[pl.ds(group * chunks + ctx, 1), :]

    return pl.pallas_call(
        kernel,
        out_shape=(
            jax.ShapeDtypeStruct((2 * groups, local_keys), jnp.float32),
            jax.ShapeDtypeStruct((2 * groups, bins), jnp.float32),
        ),
        in_specs=[VMEM] * 3,
        out_specs=(VMEM, VMEM),
        scratch_shapes=[pltpu.VMEM((rows, local_keys), jnp.float32)],
        compiler_params=pltpu.CompilerParams(vmem_limit_bytes=4 << 20),
    )(mine, theirs, edges)


def local(queries, key_states, obs_positions, block_lists, bin_edges):
    query_rows, heads_dev, head_dim = queries.shape
    local_keys, groups_dev, _ = key_states.shape
    per_group = heads_dev // groups_dev
    ctx_count = lax.axis_size("ctx")
    sub_count = lax.axis_size("sub")
    both_count = ctx_count * sub_count
    groups = groups_dev // sub_count
    sub = lax.axis_index("sub")
    ctx = lax.axis_index("ctx")
    scale = head_dim ** (-0.5)
    factor = ctx_count * local_keys / (query_rows * both_count * per_group)

    order = [2, 3, 1] if ctx_count == 4 else list(range(1, ctx_count))
    own_keys = lax.dynamic_slice_in_dim(key_states, sub * groups, groups, 1)
    own_keys = jnp.transpose(own_keys, (1, 0, 2))
    keys = [own_keys] + [
        lax.ppermute(own_keys, "ctx", xor_pairs(ctx_count, distance))
        for distance in order
    ]

    swap = xor_pairs(sub_count, 1)
    queries4 = queries.reshape(query_rows, groups_dev, per_group, head_dim)
    sibling_queries = lax.ppermute(queries4, "sub", swap)
    facts = jnp.concatenate([obs_positions, block_lists.reshape(-1)])
    both_facts = jnp.stack([facts, lax.ppermute(facts, "sub", swap)])
    positions = both_facts[:, :query_rows].reshape(-1)
    lists = both_facts[:, query_rows:]
    owners = jnp.bitwise_xor(ctx, jnp.array([0, *order], jnp.int32))
    bias = visible_bias(positions, lists, owners, local_keys)

    query_parts = []
    for part in (queries4, sibling_queries):
        part = lax.dynamic_slice_in_dim(part, sub * groups, groups, 1)
        query_parts += scaled_parts(part, scale * LOG2E)
    mass = mass_call(query_parts, keys, order, bias, factor)

    near = lax.ppermute(mass, "ctx", xor_pairs(ctx_count, 1))
    aside = lax.ppermute(mass, "sub", swap)
    across = lax.ppermute(mass, ("ctx", "sub"), xor_pairs(both_count, 3))
    mine = jnp.concatenate([mass + near, aside + across])
    theirs = None
    distance = 2
    while distance < ctx_count:
        if theirs is not None:
            mine = mine + theirs
        last = distance * 2 >= ctx_count
        pairs = xor_pairs(both_count, distance * sub_count + (1 if last else 0))
        theirs = lax.ppermute(mine, ("ctx", "sub"), pairs)
        distance *= 2
    edges = jnp.stack([bin_edges[:-1], bin_edges[1:]])
    return finish_call(mine, theirs, edges, groups, ctx_count)


def solution(mesh):
    return jax.shard_map(
        local,
        mesh=mesh,
        in_specs=(
            P(("groups", "ctx", "sub"), "kvh", None),
            P(("groups", "ctx"), "kvh", None),
            P(("groups", "ctx", "sub")),
            P(("groups", "ctx", "sub"), None),
            P("groups"),
        ),
        out_specs=(P("kvh", ("groups", "ctx")), P("kvh", "groups")),
        check_vma=False,
    )
```
